32 devices in a mesh: row: 4 (over x, core), col: 8 (over z, y).
Axes of the slice: x: 2, y: 2, z: 4, core: 2. Of those that a mesh axis runs over, the one named last changes fastest.
Arguments:
- coords: float32 [3, 524288], P(None, ('row', 'col')), may hold values from 0 to 6
- vectors: bfloat16 [64, 524288], P(None, ('row', 'col')), may hold values from -0.59765625 to 0.59765625
- basis: bfloat16 [32, 524288], P(None, ('row', 'col')), may hold values from -1.5 to 1.5
- transfer: float32 [32, 65536], P(None, ('row', 'col')), may hold values from -0.3 to 0.3
- leaf_skeleton: float32 [3, 65536], P(None, ('row', 'col')), may hold values from 0 to 6
- device_skeleton: float32 [3, 1024], P(None, ('row', 'col')), may hold values from 0 to 6
- near_pairs: int32 [2, 12288], P(None, ('row', 'col')), may hold values from 0 to 2047, as said below
- far_leaves: int32 [2048, 8], P(('row', 'col')), may hold values from 0 to 2047, as said below
- far_devices: int32 [32, 16], P(('row', 'col')), may hold values from 0 to 31
Outputs:
- product: float32 [64, 524288], P(None, ('row', 'col'))
The draws below stay inside these ranges and needn't reach their ends.
Inputs may be any that keep to these rules, and one draw needn't show every extreme that they name: `near_pairs`: device k of the row x col grid (k = row index * 8 + col index) holds near blocks k * 6 * 64 to (k + 1) * 6 * 64 - 1 and leaves k * 64 to (k + 1) * 64 - 1; the target and the source leaf of each of its near blocks lie on device k or on a device beside it in the grid, diagonals included. `far_leaves`: the coupling partners of a leaf lie on that leaf's device or on a device beside it in the row x col grid, diagonals included.
All inputs are finite; a program needn't handle non-finite values.
Results may differ from the reference program's by a relative error of at most 0.004.
Values may be sent and summed in bfloat16 or wider, within the bound.
No kernel may reach another device: no remote copies, remote signals or barrier semaphores. Data moves between devices by JAX's collectives and lax.ppermute only.
A program may use at most 256 MiB of HBM per device.

```python
import jax
import jax.numpy as jnp
from jax import lax

LEAF = 256
RANK = 32
VEC = 64
LEAF_DEV = 64
NEAR = 6
FAR_LEAF = 8
FAR_DEV = 16
NLEAF = 2048
NPTS = 524288
NBLK = 12288
N_ROW = 4
N_COL = 8


def neighbour_leaf(key, owner_dev, stay, crowded):
    key_row = jax.random.fold_in(key, 1)
    key_col = jax.random.fold_in(key, 2)
    key_first = jax.random.fold_in(key, 3)
    key_second = jax.random.fold_in(key, 4)
    count = owner_dev.shape
    row_here = owner_dev // N_COL
    col_here = owner_dev % N_COL
    row_there = jnp.clip(row_here + jax.random.randint(key_row, count, -1, 2), 0, N_ROW - 1)
    col_there = jnp.clip(col_here + jax.random.randint(key_col, count, -1, 2), 0, N_COL - 1)
    row_there = jnp.where(stay > 0, row_here, row_there)
    col_there = jnp.where(stay > 0, col_here, col_there)
    leaf_first = jax.random.randint(key_first, count, 0, LEAF_DEV)
    if crowded:
        leaf_second = jax.random.randint(key_second, count, 0, LEAF_DEV)
        leaf_first = jnp.minimum(leaf_first, leaf_second)
    return (row_there * N_COL + col_there) * LEAF_DEV + leaf_first


def draw_near_pairs(key, part):
    block_dev = jnp.arange(NBLK, dtype=jnp.int32) // (NEAR * LEAF_DEV)
    stay = jax.random.randint(jax.random.fold_in(key, 13), (NBLK,), 0, 2)
    target = neighbour_leaf(jax.random.fold_in(key, 11), block_dev, stay, True)
    source = neighbour_leaf(jax.random.fold_in(key, 12), block_dev, jnp.zeros_like(stay), False)
    return jnp.stack([target, source]).astype(jnp.int32)


def draw_far_leaves(key, part):
    leaf_dev = jnp.arange(NLEAF * FAR_LEAF, dtype=jnp.int32) // (FAR_LEAF * LEAF_DEV)
    stay = jnp.zeros_like(leaf_dev)
    chosen = neighbour_leaf(jax.random.fold_in(key, 21), leaf_dev, stay, False)
    return chosen.reshape(NLEAF, FAR_LEAF).astype(jnp.int32)


def touch_ends(array, rng, smallest, largest):
    extent = array.shape
    place = [jax.random.randint(jax.random.fold_in(rng, axis), (), 0, extent[axis]) for axis in range(len(extent))]
    array = array.at[tuple(place)].set(smallest)
    longest = extent.index(max(extent))
    place[longest] = (place[longest] + 1) % extent[longest]
    return array.at[tuple(place)].set(largest)


def shard_levels(stream_key, dims, shards, low, largest):
    factor_of, own = 1.0, jax.random.fold_in(stream_key, 6)
    for position, shards_of in shards:
        draws = jnp.exp(jax.random.uniform(jax.random.fold_in(own, position), (shards_of,), jnp.float32, low / len(shards), largest / len(shards)))
        factor_of = factor_of * jnp.repeat(draws, dims[position] // shards_of).reshape([-1 if axis == position else 1 for axis in range(len(dims))])
    return factor_of


def scatter_about(key, shape, spread, reach, shards=(), kind=jnp.bfloat16):
    result = spread * jax.random.normal(key, shape, jnp.float32)
    if shards:
        result = result * shard_levels(key, shape, shards, -0.22, 0.18)
    return jnp.clip(result, -reach, reach).astype(kind)


def setup_inputs(seed: int = 0) -> dict:
    key_of = jax.random.split(jax.random.key(seed), 10)
    return {
        "coords": jnp.clip(6.0 * jax.random.uniform(key_of[0], (3, NPTS), jnp.float32) ** shard_levels(key_of[0], (3, NPTS), ((1, 32),), -0.2, 0.2), 0.0, 6.0),
        "vectors": scatter_about(key_of[1], (VEC, NPTS), 0.1, 0.59765625, ((1, 32),)),
        "basis": scatter_about(key_of[2], (RANK, NPTS), 0.25, 1.5, ((1, 32),)),
        "transfer": scatter_about(key_of[3], (RANK, NLEAF * RANK), 0.05, 0.3, ((1, 32),), jnp.float32),
        "leaf_skeleton": jnp.clip(6.0 * jax.random.uniform(key_of[4], (3, NLEAF * RANK), jnp.float32) ** shard_levels(key_of[4], (3, NLEAF * RANK), ((1, 32),), -0.2, 0.2), 0.0, 6.0),
        "device_skeleton": jnp.clip(6.0 * jax.random.uniform(key_of[5], (3, N_ROW * N_COL * RANK), jnp.float32) ** shard_levels(key_of[5], (3, N_ROW * N_COL * RANK), ((1, 32),), -0.2, 0.2), 0.0, 6.0),
        "near_pairs": draw_near_pairs(jax.random.fold_in(key_of[9], 71), 0),
        "far_leaves": draw_far_leaves(jax.random.fold_in(key_of[9], 71), 0),
        "far_devices": touch_ends(jax.random.randint(key_of[8], (N_ROW * N_COL, FAR_DEV), 0, N_ROW * N_COL), jax.random.fold_in(key_of[8], 1), 0, (N_ROW * N_COL) - 1).astype(jnp.int32),
    }


HIGH = lax.Precision.HIGHEST


def kernel_block(left, right):
    total = None
    for dimension in range(3):
        gap = left[..., dimension, :, None] - right[..., dimension, None, :]
        total = gap * gap if total is None else total + gap * gap
    return jnp.exp(-0.5 * total)


def reference(coords, vectors, basis, transfer, leaf_skeleton, device_skeleton, near_pairs, far_leaves, far_devices):
    devices = N_ROW * N_COL
    coords_leaf = coords.reshape(3, NLEAF, LEAF)
    vectors_leaf = vectors.reshape(VEC, NLEAF, LEAF)
    pairs = near_pairs.reshape(2, devices, NEAR * LEAF_DEV)

    def near_step(total, pair):
        target, source = pair
        tgt_points = jnp.transpose(coords_leaf[:, target], (1, 0, 2))
        src_points = jnp.transpose(coords_leaf[:, source], (1, 0, 2))
        block = kernel_block(tgt_points, src_points).astype(jnp.bfloat16)
        src_vectors = vectors_leaf[:, source].astype(jnp.float32)
        partial_value = jnp.einsum("vbs,bts->bvt", src_vectors, block.astype(jnp.float32), precision=HIGH)
        return total.at[target].add(partial_value), None

    start = jnp.zeros((NLEAF, VEC, LEAF), jnp.float32)
    near_total, _ = lax.scan(near_step, start, (pairs[0], pairs[1]))
    near_field = jnp.transpose(near_total, (1, 0, 2)).reshape(VEC, NPTS)

    basis_leaf = basis.reshape(RANK, NLEAF, LEAF)
    coeff = jnp.einsum("vnl,rnl->vnr", vectors_leaf.astype(jnp.float32), basis_leaf.astype(jnp.float32), precision=HIGH).astype(jnp.bfloat16)
    transfer_mats = transfer.reshape(RANK, NLEAF, RANK)
    coeff_dev = coeff.astype(jnp.float32).reshape(VEC, devices, LEAF_DEV, RANK)
    device_coeff = jnp.einsum("vdir,rdis->vds", coeff_dev, transfer_mats.reshape(RANK, devices, LEAF_DEV, RANK), precision=HIGH)

    skeleton_leaf = leaf_skeleton.reshape(3, NLEAF, RANK)

    def leaf_block(item):
        lists, own_skel = item
        picked = jnp.transpose(coeff[:, lists].astype(jnp.float32), (1, 2, 0, 3))
        picked_skel = jnp.transpose(skeleton_leaf[:, lists], (1, 2, 0, 3))
        coupling = kernel_block(picked_skel, own_skel[:, None])
        return jnp.einsum("ifvs,ifst->ivt", picked, coupling, precision=HIGH)

    own_skeleton = jnp.transpose(skeleton_leaf, (1, 0, 2)).reshape(devices, LEAF_DEV, 3, RANK)
    leaf_far = lax.map(leaf_block, (far_leaves.reshape(devices, LEAF_DEV, FAR_LEAF), own_skeleton))
    leaf_far = leaf_far.reshape(NLEAF, VEC, RANK)

    skeleton_dev = device_skeleton.reshape(3, devices, RANK)
    picked_coeff = device_coeff[:, far_devices]
    picked_skel = jnp.transpose(skeleton_dev[:, far_devices], (1, 2, 0, 3))
    own_dev_skel = jnp.transpose(skeleton_dev, (1, 0, 2))
    coupling_top = kernel_block(picked_skel, own_dev_skel[:, None])
    device_far = jnp.einsum("vdfs,dfst->dvt", picked_coeff, coupling_top, precision=HIGH)

    device_of_leaf = jnp.repeat(device_far, LEAF_DEV, axis=0)
    field = leaf_far + jnp.einsum("nvs,rns->nvr", device_of_leaf, transfer_mats, precision=HIGH)
    field = field.astype(jnp.bfloat16)
    far_part = jnp.einsum("nvr,rnl->vnl", field.astype(jnp.float32), basis_leaf.astype(jnp.float32), precision=HIGH)
    return near_field + far_part.reshape(VEC, NPTS)
```

```python
import functools

import jax
import jax.numpy as jnp
from jax import lax
from jax.experimental import pallas as pl
from jax.experimental.pallas import tpu as pltpu
from jax.sharding import PartitionSpec as P

HIGH = lax.Precision.HIGHEST
F32, BF16, I32 = jnp.float32, jnp.bfloat16, jnp.int32
CAP = 40
SHIFT = 4096
SMEM = pl.BlockSpec(memory_space=pltpu.SMEM)
VMEM = pl.BlockSpec(memory_space=pltpu.VMEM)
ANY = pl.BlockSpec(memory_space=pl.ANY)


def params(**more):
    return pltpu.CompilerParams(vmem_limit_bytes=60000 * 1024, **more)


def shift(block, axis, step):
    devices = range(lax.axis_size(axis))
    route = [(i, i + step) for i in devices if i + step in devices]
    return lax.ppermute(block, axis, route)


def gather_all(block, axes):
    count = lax.axis_size(axes)
    have, held = 1, block[None]
    while have < count:
        take = min(have, count - have)
        route = [(i, (i - have) % count) for i in range(count)]
        held = jnp.concatenate([held, lax.ppermute(held[:take], axes, route)])
        have += take
    return held


def kernel_block(left, right):
    total = None
    for dimension in range(3):
        gap = left[..., dimension, :, None] - right[..., dimension, None, :]
        total = gap * gap if total is None else total + gap * gap
    return jnp.exp(-0.5 * total)


def plan_kernel(cols, leaves, place, own, left, right, lists, counts, relay, slots):
    row, col = place[0], place[1]
    pairs = own.shape[1]
    for i in range(counts.shape[0]):
        counts[i] = 0

    @pl.loop(0, slots.shape[0])
    def _(i):
        slots[i] = -1

    @pl.loop(0, relay.shape[1])
    def _(i):
        relay[0, i] = 0
        relay[1, i] = 0

    def split(leaf):
        owner = leaf // leaves
        return owner // cols - row, owner % cols - col, leaf % leaves

    def put(which, value):
        at = counts[which]
        lists[which, at] = value
        counts[which] = at + 1

    def slot_of(table, counter, key):
        at = table * 3 * leaves + key
        fresh = slots[at] < 0

        @pl.when(fresh)
        def _():
            slots[at] = counts[counter]
            counts[counter] = counts[counter] + 1

        return slots[at], fresh

    def scan(ref, side):
        @pl.loop(0, pairs)
        def _(p):
            t_row, t_col, t_leaf = split(ref[0, p])
            s_row, s_col, s_leaf = split(ref[1, p])
            target = (t_row + 1) * leaves + t_leaf
            source = (s_row + 1) * leaves + s_leaf
            here = t_col == 0
            near = here & (s_col == 0)
            beside = here & ((s_col == 1) | (s_col == -1))
            which = jnp.where(near, 0, jnp.where(beside, jnp.where(s_row == 0, 1, 2), 4))
            packed = target * SHIFT + source + jnp.where(s_col == 1, 3 * leaves, 0)
            put(which, packed)
            if side == 0:
                for way, step in ((0, 1), (1, -1)):

                    @pl.when((t_col == step) & (s_col == -step))
                    def _():
                        at, fresh = slot_of(way, 5 + way, source)

                        @pl.when(fresh)
                        def _():
                            relay[way, at] = source
            else:
                way = 0 if side == -1 else 1

                @pl.when(here & (s_col == 2 * side))
                def _():
                    at, _ = slot_of(2 + way, 7 + way, source)
                    put(3, target * SHIFT + way * 2048 + at)

    scan(own, 0)

    @pl.when(col > 0)
    def _():
        scan(left, -1)

    @pl.when(col < cols - 1)
    def _():
        scan(right, 1)


def plan(place, own, left, right, cols, leaves):
    pairs = own.shape[1]
    return pl.pallas_call(
        functools.partial(plan_kernel, cols, leaves),
        out_shape=(
            jax.ShapeDtypeStruct((5, 3 * pairs), I32),
            jax.ShapeDtypeStruct((16,), I32),
            jax.ShapeDtypeStruct((2, pairs + CAP), I32),
        ),
        in_specs=[SMEM] * 4,
        out_specs=(SMEM, SMEM, SMEM),
        scratch_shapes=[pltpu.SMEM((4 * 3 * leaves,), I32)],
        name="plan",
    )(place, own, left, right)


def pair_value(points_s, points_t, rows):
    width = points_s.shape[1]
    columns = points_s.T
    parts = []
    for start in range(0, width, 64):
        total = None
        for axis in range(3):
            gap = columns[start : start + 64, axis : axis + 1] - points_t[axis : axis + 1, :]
            total = gap * gap if total is None else total + gap * gap
        parts.append(jnp.exp(-0.5 * total).astype(BF16))
    block = jnp.concatenate(parts, axis=0)
    return jnp.dot(rows, block, preferred_element_type=F32)


def near_kernel(which, leaves, fresh, *refs):
    lists, counts, *refs = refs
    if not fresh:
        start, *refs = refs
    targets, sources, *refs = refs
    pools = refs[:-3]
    out, pool, sems = refs[-3:]
    width = targets.shape[2] // leaves
    copies = [pltpu.make_async_copy(pools[i], pool.at[i], sems.at[i]) for i in range(len(pools))]
    for copy in copies:
        copy.start()
    if fresh:
        for i in range(3):
            out[i] = jnp.zeros(out.shape[1:], F32)
    else:
        for i in range(3):
            out[i] = start[i]
    for copy in copies:
        copy.wait()

    def spot(flat):
        return flat // leaves, pl.ds(pl.multiple_of((flat % leaves) * width, width), width)

    count = counts[which]

    @pl.loop(0, (count + 1) // 2)
    def _(step):
        values = []
        for i in range(2):
            packed = lists[which, jnp.minimum(step * 2 + i, count - 1)]
            t_part, t_span = spot(packed // SHIFT)
            s_part, s_span = spot(packed % SHIFT)
            value = pair_value(
                sources[s_part, :, s_span], targets[t_part, :, t_span], pool[s_part, :, s_span]
            )
            values.append((t_part, t_span, value))
        t_part, t_span, value = values[0]
        out[t_part, :, t_span] += value

        @pl.when(step * 2 + 1 < count)
        def _():
            t_part, t_span, value = values[1]
            out[t_part, :, t_span] += value


def near(which, leaves, lists, counts, start, targets, sources, pools):
    rows, points = pools[0].shape
    first = [] if start is None else [start]
    return pl.pallas_call(
        functools.partial(near_kernel, which, leaves, start is None),
        out_shape=jax.ShapeDtypeStruct((3, rows, points), F32),
        in_specs=[SMEM, SMEM] + [VMEM] * (len(first) + 2) + [ANY] * len(pools),
        out_specs=VMEM,
        scratch_shapes=[
            pltpu.VMEM((len(pools), rows, points), BF16),
            pltpu.SemaphoreType.DMA((len(pools),)),
        ],
        compiler_params=params(),
        name="near%d" % which,
    )(lists, counts, *first, targets, sources, *pools)


def relay_kernel(leaves, base, relay, points, *refs):
    pools, (rows_out, points_out, sems) = refs[:6], refs[6:]
    width = points.shape[2] // leaves
    begin = base[0]

    def spot(flat):
        return flat // leaves, pl.ds(pl.multiple_of((flat % leaves) * width, width), width)

    def copy(way, i, part, span):
        return pltpu.make_async_copy(
            pools[way * 3 + part].at[:, span], rows_out.at[way, i], sems.at[way, i]
        )

    for way in range(2):

        @pl.loop(0, CAP)
        def _(i):
            flat = relay[way, begin + i]
            part, span = spot(flat)
            for option in range(3):

                @pl.when(part == option)
                def _():
                    copy(way, i, option, span).start()

            points_out[way, i] = points[way * 3 + part, :, span]

    for way in range(2):

        @pl.loop(0, CAP)
        def _(i):
            copy(way, i, 0, pl.ds(0, width)).wait()


def relays(leaves, base, relay, points, pools):
    rows, length = pools[0].shape
    width = length // leaves
    return pl.pallas_call(
        functools.partial(relay_kernel, leaves),
        out_shape=(
            jax.ShapeDtypeStruct((2, CAP, rows, width), BF16),
            jax.ShapeDtypeStruct((2, CAP, 8, width), F32),
        ),
        in_specs=[SMEM, SMEM, VMEM] + [ANY] * 6,
        out_specs=(VMEM, VMEM),
        scratch_shapes=[pltpu.SemaphoreType.DMA((2, CAP))],
        compiler_params=params(),
        name="relays",
    )(base, relay, points, *pools)


def late_kernel(leaves, base, lists, counts, start, targets, points, rows, out):
    width = targets.shape[2] // leaves
    for i in range(3):
        out[i] = start[i]
    begin = base[0]

    @pl.loop(0, counts[3])
    def _(step):
        packed = lists[3, step]
        flat = packed // SHIFT
        t_part = flat // leaves
        t_span = pl.ds(pl.multiple_of((flat % leaves) * width, width), width)
        way = (packed % SHIFT) // 2048
        slot = packed % 2048 - begin

        @pl.when((slot >= 0) & (slot < CAP))
        def _():
            out[t_part, :, t_span] += pair_value(
                points[way, slot], targets[t_part, :, t_span], rows[way, slot]
            )


def late(leaves, base, lists, counts, start, targets, points, rows):
    return pl.pallas_call(
        functools.partial(late_kernel, leaves),
        out_shape=jax.ShapeDtypeStruct(start.shape, F32),
        in_specs=[SMEM] * 3 + [VMEM] * 4,
        out_specs=VMEM,
        compiler_params=params(),
        name="late",
    )(base, lists, counts, start, targets, points, rows)


def shards(
    coords,
    vectors,
    basis,
    transfer,
    leaf_skeleton,
    device_skeleton,
    near_pairs,
    far_leaves,
    far_devices,
):
    col_count = lax.axis_size("col")
    row_here = lax.axis_index("row")
    col_here = lax.axis_index("col")
    rank_size = basis.shape[0]
    vec_count, points = vectors.shape
    leaves = transfer.shape[1] // rank_size
    leaf_width = points // leaves

    pairs_left, pairs_right = shift(near_pairs, "col", 1), shift(near_pairs, "col", -1)
    vec_left, vec_right = shift(vectors, "col", 1), shift(vectors, "col", -1)
    vec_up, vec_down = shift(vectors, "row", 1), shift(vectors, "row", -1)
    extra = jnp.concatenate([coords, leaf_skeleton], axis=1)
    extra = jnp.stack([shift(extra, "col", 1), extra, shift(extra, "col", -1)])
    extra = jnp.stack([shift(extra, "row", 1), extra, shift(extra, "row", -1)])
    place = jnp.stack([row_here, col_here]).astype(I32)
    lists, counts, relay = plan(place, near_pairs, pairs_left, pairs_right, col_count, leaves)
    spots = jnp.pad(extra[..., :points], ((0, 0), (0, 0), (0, 5), (0, 0)))
    middle = spots[:, 1]
    sides = jnp.concatenate([spots[:, 0], spots[:, 2]])

    coeff_own = jnp.einsum(
        "vil,ril->vir",
        vectors.reshape(vec_count, leaves, leaf_width),
        basis.reshape(rank_size, leaves, leaf_width),
        preferred_element_type=F32,
    ).astype(BF16)
    coeff = coeff_own.reshape(vec_count, leaves * rank_size)
    coeff = jnp.stack([shift(coeff, "col", 1), coeff, shift(coeff, "col", -1)])
    coeff = jnp.stack([shift(coeff, "row", 1), coeff, shift(coeff, "row", -1)])

    total = near(0, leaves, lists, counts, None, middle, middle, [vec_up, vectors, vec_down])

    transfer_mats = transfer.reshape(rank_size, leaves, rank_size)
    device_coeff = jnp.einsum(
        "vir,ris->vs", coeff_own.astype(F32), transfer_mats, precision=HIGH
    )
    rounds_here = (jnp.maximum(counts[5], counts[6]) + CAP - 1) // CAP
    sheet = jnp.concatenate(
        [
            device_coeff,
            device_skeleton,
            jnp.full((1, rank_size), rounds_here, F32),
        ]
    )
    sheets = gather_all(sheet, ("row", "col"))
    devices = sheets.shape[0]
    rounds = jnp.max(sheets[:, vec_count + 3, 0]).astype(I32)
    me = row_here * col_count + col_here
    chosen = sheets[(far_devices[0] - me) % devices]
    coupling_top = kernel_block(chosen[:, vec_count : vec_count + 3], device_skeleton[None])
    device_far = jnp.einsum("fvs,fst->vt", chosen[:, :vec_count], coupling_top, precision=HIGH)

    coeff_pad = coeff.reshape(9, vec_count, leaves, rank_size)
    skeleton_pool = extra[..., points:].reshape(9, 3, leaves, rank_size)
    owner = far_leaves // leaves
    far_hood = (owner // col_count - row_here + 1) * 3 + owner % col_count - col_here + 1
    far_leaf = far_leaves % leaves
    picked_coeff = coeff_pad[far_hood, :, far_leaf, :].astype(F32)
    picked_skel = skeleton_pool[far_hood, :, far_leaf, :]
    own_skel = jnp.transpose(leaf_skeleton.reshape(3, leaves, rank_size), (1, 0, 2))
    coupling = kernel_block(picked_skel, own_skel[:, None])
    leaf_far = jnp.einsum("ifvs,ifst->ivt", picked_coeff, coupling, precision=HIGH)
    field = leaf_far + jnp.einsum("vs,ris->ivr", device_far, transfer_mats, precision=HIGH)
    far_part = jnp.einsum(
        "ivr,ril->vil",
        field.astype(BF16),
        basis.reshape(rank_size, leaves, leaf_width),
        preferred_element_type=F32,
    ).reshape(vec_count, points)

    pools = [
        shift(vec_left, "row", 1),
        vec_left,
        shift(vec_left, "row", -1),
        shift(vec_right, "row", 1),
        vec_right,
        shift(vec_right, "row", -1),
    ]
    total = near(1, leaves, lists, counts, total, middle, sides, pools)
    total = near(2, leaves, lists, counts, total, middle, sides, pools)

    def relay_round(index, total):
        base = (index * CAP).reshape(1)
        rows, spots = relays(leaves, base, relay, sides, pools)
        rows = jnp.stack([shift(rows[0], "col", 1), shift(rows[1], "col", -1)])
        spots = jnp.stack([shift(spots[0], "col", 1), shift(spots[1], "col", -1)])
        return late(leaves, base, lists, counts, total, middle, spots, rows)

    total = relay_round(jnp.zeros((), I32), total)
    _, total = lax.while_loop(
        lambda state: state[0] < rounds,
        lambda state: (state[0] + 1, relay_round(*state)),
        (jnp.ones((), I32), total),
    )
    from_below = shift(total[0].astype(BF16), "row", -1)
    from_above = shift(total[2].astype(BF16), "row", 1)
    return total[1] + from_below.astype(F32) + from_above.astype(F32) + far_part


def solution(mesh):
    spread = P(None, ("row", "col"))
    lists = P(("row", "col"), None)
    in_specs = (spread,) * 7 + (lists,) * 2
    return jax.shard_map(
        shards, mesh=mesh, in_specs=in_specs, out_specs=spread, check_vma=False
    )
```

```python
import functools
import math

import jax
import jax.numpy as jnp
from jax import lax
from jax.experimental import pallas as pl
from jax.experimental.pallas import tpu as pltpu
from jax.sharding import PartitionSpec as P

HIGH = lax.Precision.HIGHEST
F32, BF16, I32 = jnp.float32, jnp.bfloat16, jnp.int32
CAP = 40
GROUP = 4
SHIFT = 4096
SMEM = pl.BlockSpec(memory_space=pltpu.SMEM)
VMEM = pl.BlockSpec(memory_space=pltpu.VMEM)
ANY = pl.BlockSpec(memory_space=pl.ANY)


def params(**more):
    return pltpu.CompilerParams(vmem_limit_bytes=58 * 1024 * 1024, **more)


def shift(block, axis, step):
    devices = range(lax.axis_size(axis))
    route = [(i, i + step) for i in devices if i + step in devices]
    return lax.ppermute(block, axis, route)


def exchange(block, axis):
    return shift(block, axis, 1), shift(block, axis, -1)


def gather_all(block, axes):
    count = lax.axis_size(axes)
    have, held = 1, block[None]
    while have < count:
        take = min(have, count - have)
        route = [(i, (i - have) % count) for i in range(count)]
        held = jnp.concatenate([held, lax.ppermute(held[:take], axes, route)])
        have += take
    return held


def kernel_block(left, right):
    total = None
    for dimension in range(3):
        gap = left[..., dimension, :, None] - right[..., dimension, None, :]
        total = gap * gap if total is None else total + gap * gap
    return jnp.exp(-0.5 * total)


def scaled(points):
    shifted = (points - 3.0) * math.sqrt(math.log2(math.e))
    return jnp.concatenate([shifted, jnp.zeros((8 - points.shape[0], points.shape[1]), F32)])


def split_rows(points, target):
    row = lax.broadcasted_iota(I32, points.shape, 0)
    half = -0.5 * jnp.sum(points * points, axis=0, keepdims=True)
    norm_row, one_row = (4, 3) if target else (3, 4)
    rest = jnp.where(row == norm_row, half, jnp.where(row == one_row, 1.0, points))
    parts = []
    for _ in range(3):
        part = rest.astype(BF16).astype(F32)
        rest = rest - part
        parts.append(part)
    high, middle, low = parts
    if target:
        order = (high, middle, low, high, middle, high)
    else:
        order = (high, high, high, middle, middle, low)
    return jnp.concatenate(order).astype(BF16)


def decode(pairs, side, row, col, cols, leaves):
    target, source = pairs[0].astype(I32), pairs[1].astype(I32)

    def split(leaf):
        owner = leaf // leaves
        return owner // cols - row, owner % cols - col, leaf % leaves

    t_row, t_col, t_leaf = split(target)
    s_row, s_col, s_leaf = split(source)
    into = (t_row + 1) * leaves + t_leaf
    out = (s_row + 1) * leaves + s_leaf
    exists = (col + side >= 0) & (col + side < cols)
    here = (t_col == 0) & exists
    beside = jnp.abs(s_col) == 1
    which = jnp.where(s_col == 0, 0, jnp.where(beside, jnp.where(s_row == 0, 1, 2), 4))
    if side == 0:
        which = jnp.where(here, which, 4)
        way = jnp.where((t_col == 1) & (s_col == -1), 0, -1)
        way = jnp.where((t_col == -1) & (s_col == 1), 1, way)
    else:
        far = here & (s_col == 2 * side)
        which = jnp.where(here, jnp.where(far, 4, which), 4)
        way = jnp.where(far, 2 if side == -1 else 3, -1)
    side_of = jnp.where(s_col == 1, 1, 0)
    part = jnp.where(which == 0, s_row + 1, side_of)
    part = jnp.where(which == 2, 2 * side_of + jnp.where(s_row == 1, 1, 0), part)
    entry = into * SHIFT + part * leaves + s_leaf
    key = jnp.where(way < 0, -1, way * 3 * leaves + out)
    return which, entry, key


def plan_kernel(leaves, which, entries, keys, lists, counts, relay, slots):
    pairs = entries.shape[0]
    reach = relay.shape[0] // 2

    def fill(ref, value):
        @pl.loop(0, ref.shape[0], unroll=8)
        def _(i):
            ref[i] = value

    fill(slots, -1)
    fill(relay, 0)

    def sort(p, found):
        group = which[p]
        at = jnp.where(group == 0, found[0], jnp.where(group == 1, found[1], found[2]))
        lists[group * pairs + at] = entries[p]
        return tuple(found[i] + jnp.where(group == i, 1, 0) for i in range(3))

    found = lax.fori_loop(0, pairs, sort, (0, 0, 0), unroll=8)
    for i in range(3):
        counts[i] = found[i]
    for i in range(3, counts.shape[0]):
        counts[i] = 0

    def note(p):
        key = keys[p]

        @pl.when(key >= 0)
        def _():
            way = lax.div(key, 3 * leaves)
            fresh = slots[key] < 0

            @pl.when(fresh)
            def _():
                slot = counts[5 + way]
                slots[key] = slot
                counts[5 + way] = slot + 1

                @pl.when(way < 2)
                def _():
                    relay[way * reach + slot] = lax.rem(key, 3 * leaves)

            @pl.when(way >= 2)
            def _():
                last = counts[3]
                target = lax.div(entries[p], SHIFT)
                lists[3 * pairs + last] = target * SHIFT + (way - 2) * 2048 + slots[key]
                counts[3] = last + 1

    @pl.loop(0, pairs, step=8)
    def _(p):
        top = keys[p]
        for i in range(1, 8):
            top = jnp.maximum(top, keys[p + i])

        @pl.when(top >= 0)
        def _():
            for i in range(8):
                note(p + i)


def plan(which, entries, keys, leaves):
    pairs = entries.shape[0]
    return pl.pallas_call(
        functools.partial(plan_kernel, leaves),
        out_shape=(
            jax.ShapeDtypeStruct((5 * pairs,), I32),
            jax.ShapeDtypeStruct((16,), I32),
            jax.ShapeDtypeStruct((2 * (pairs + CAP),), I32),
        ),
        in_specs=[SMEM] * 3,
        out_specs=(SMEM, SMEM, SMEM),
        scratch_shapes=[pltpu.SMEM((4 * 3 * leaves,), I32)],
        cost_estimate=pl.CostEstimate(flops=10**10, bytes_accessed=10**5, transcendentals=0),
        name="plan",
    )(which, entries, keys)


def pipeline(count, total, make, take, blocks):
    @pl.when(count > 0)
    def _():
        def fill(group, buffers):
            for i in range(GROUP):
                buffers[i] = make(jnp.minimum(group * GROUP + i, count - 1))

        def drain(group, buffers):
            values = []
            for i in range(GROUP):
                index = group * GROUP + i
                rows, spot, keep = take(jnp.minimum(index, count - 1))
                keep = jnp.where(index < count, keep, 0.0)
                value = jnp.dot(rows, buffers[i], preferred_element_type=F32)
                values.append((spot, value * keep))
            for (part, span), value in values:
                total[part, :, span] += value

        even, odd = blocks
        fill(0, even)

        @pl.loop(0, (count + 2 * GROUP - 1) // (2 * GROUP))
        def _(step):
            fill(2 * step + 1, odd)
            drain(2 * step, even)
            fill(2 * step + 2, even)
            drain(2 * step + 1, odd)


def spot_of(flat, leaves, width):
    return lax.div(flat, leaves), pl.ds(pl.multiple_of(lax.rem(flat, leaves) * width, width), width)


def matrix(source, target):
    exponent = lax.dot_general(
        source, target, (((0,), (0,)), ((), ())), preferred_element_type=F32
    )
    return jnp.exp2(exponent).astype(BF16)


def features(points, spots, out, target, leaves):
    width = out.shape[2] // leaves

    @pl.loop(0, leaves)
    def _(leaf):
        span = pl.ds(pl.multiple_of(leaf * width, width), width)
        for i, (row, col) in enumerate(spots):
            out[i, :, span] = split_rows(scaled(points[row, col, :, span]), target)


OWN_COL = ((0, 1), (1, 1), (2, 1))


def near_kernel(which, leaves, spots, fresh, *refs):
    lists, counts, *refs = refs
    if not fresh:
        start, *refs = refs
    points, *refs = refs
    pools = refs[:-7]
    out, pool, sources, targets, sems, *blocks = refs[-7:]
    length = pool.shape[2]
    width = length // leaves
    many = len(pools)
    copies = [pltpu.make_async_copy(pools[i], pool.at[i], sems.at[i]) for i in range(many)]
    if not fresh:
        copies.append(pltpu.make_async_copy(start, out, sems.at[many]))
    for copy in copies:
        copy.start()
    features(points, OWN_COL, targets, True, leaves)
    features(points, spots, sources, False, leaves)
    if fresh:

        @pl.loop(0, leaves)
        def _(leaf):
            span = pl.ds(pl.multiple_of(leaf * width, width), width)
            for i in range(3):
                out[i, :, span] = jnp.zeros((out.shape[1], width), F32)

    for copy in copies:
        copy.wait()
    begin = which * (lists.shape[0] // 5)

    def make(i):
        packed = lists[begin + i]
        t_part, t_span = spot_of(lax.div(packed, SHIFT), leaves, width)
        s_part, s_span = spot_of(lax.rem(packed, SHIFT), leaves, width)
        return matrix(sources[s_part, :, s_span], targets[t_part, :, t_span])

    def take(i):
        packed = lists[begin + i]
        s_part, s_span = spot_of(lax.rem(packed, SHIFT), leaves, width)
        return pool[s_part, :, s_span], spot_of(lax.div(packed, SHIFT), leaves, width), 1.0

    pipeline(counts[which], out, make, take, blocks)


def block_scratch(width):
    return [pltpu.VMEM((GROUP, width, width), BF16)] * 2


def near(which, leaves, spots, lists, counts, start, points, pools, cost):
    rows, length = pools[0].shape
    many = len(pools)
    first = [] if start is None else [start]
    return pl.pallas_call(
        functools.partial(near_kernel, which, leaves, spots, start is None),
        out_shape=jax.ShapeDtypeStruct((3, rows, length), F32),
        in_specs=[SMEM, SMEM] + [ANY] * len(first) + [VMEM] + [ANY] * many,
        out_specs=VMEM,
        scratch_shapes=[
            pltpu.VMEM((many, rows, length), BF16),
            pltpu.VMEM((many, 48, length), BF16),
            pltpu.VMEM((3, 48, length), BF16),
            pltpu.SemaphoreType.DMA((many + 1,)),
        ]
        + block_scratch(length // leaves),
        compiler_params=params(),
        cost_estimate=pl.CostEstimate(flops=cost, bytes_accessed=3 * 10**7, transcendentals=0),
    )(lists, counts, *first, points, *pools)


def relay_kernel(leaves, base, relay, points, *refs):
    pools, (rows_out, sems) = refs[:6], refs[6:]
    height, length = pools[0].shape
    width = length // leaves
    begin = base[0]
    reach = relay.shape[0] // 2

    def copy(way, i, part, span):
        return pltpu.make_async_copy(
            pools[way * 3 + part].at[:, span], rows_out.at[way, i, :height], sems.at[way, i]
        )

    for way in range(2):

        @pl.loop(0, CAP)
        def _(i):
            part, span = spot_of(relay[way * reach + begin + i], leaves, width)
            for option in range(3):

                @pl.when(part == option)
                def _():
                    copy(way, i, option, span).start()

            rest = scaled(points[part, 2 * way, :, span])
            parts = []
            for _ in range(3):
                parts.append(rest.astype(BF16).astype(F32))
                rest = rest - parts[-1]
            high = parts[0] + pltpu.roll(parts[2], 5, 0)
            rows_out[way, i, height:] = jnp.concatenate([high, parts[1]]).astype(BF16)

    for way in range(2):

        @pl.loop(0, CAP)
        def _(i):
            copy(way, i, 0, pl.ds(0, width)).wait()


def relays(leaves, base, relay, points, pools):
    height, length = pools[0].shape
    width = length // leaves
    return pl.pallas_call(
        functools.partial(relay_kernel, leaves),
        out_shape=jax.ShapeDtypeStruct((2, CAP, height + 16, width), BF16),
        in_specs=[SMEM, SMEM, VMEM] + [ANY] * 6,
        out_specs=VMEM,
        scratch_shapes=[pltpu.SemaphoreType.DMA((2, CAP))],
        compiler_params=params(),
        name="relays",
    )(base, relay, points, *pools)


def late_kernel(leaves, base, lists, counts, start, points, *refs):
    arrived, (out, sources, targets, sem, *blocks) = refs[:2], refs[2:]
    height, length = out.shape[1:]
    width = length // leaves
    copy = pltpu.make_async_copy(start, out, sem)
    copy.start()
    features(points, OWN_COL, targets, True, leaves)
    for way in range(2):

        @pl.loop(0, CAP)
        def _(i):
            rows = arrived[way][i, height:].astype(F32)
            high, middle = rows[:8], rows[8:]
            row = lax.broadcasted_iota(I32, high.shape, 0)
            low = pltpu.roll(high, 3, 0)
            exact = jnp.where(row < 3, high + middle + low, 0.0)
            sources[way, i] = split_rows(exact, False)

    copy.wait()
    begin = base[0]
    skip = 3 * (lists.shape[0] // 5)

    def slot_of(packed):
        slot = lax.rem(packed, 2048) - begin
        inside = jnp.clip(slot, 0, CAP - 1)
        return lax.div(lax.rem(packed, SHIFT), 2048), inside, jnp.where(slot == inside, 1.0, 0.0)

    def make(i):
        packed = lists[skip + i]
        way, slot, _ = slot_of(packed)
        t_part, t_span = spot_of(lax.div(packed, SHIFT), leaves, width)
        return matrix(sources[way, slot], targets[t_part, :, t_span])

    def take(i):
        packed = lists[skip + i]
        way, slot, keep = slot_of(packed)
        rows = jnp.where(way == 0, arrived[0][slot, :height], arrived[1][slot, :height])
        return rows, spot_of(lax.div(packed, SHIFT), leaves, width), keep

    pipeline(counts[3], out, make, take, blocks)


def late(leaves, base, lists, counts, start, points, arrived):
    width = start.shape[2] // leaves
    return pl.pallas_call(
        functools.partial(late_kernel, leaves),
        out_shape=jax.ShapeDtypeStruct(start.shape, F32),
        in_specs=[SMEM] * 3 + [ANY] + [VMEM] * 3,
        out_specs=VMEM,
        scratch_shapes=[
            pltpu.VMEM((2, CAP, 48, width), BF16),
            pltpu.VMEM((3, 48, start.shape[2]), BF16),
            pltpu.SemaphoreType.DMA,
        ]
        + block_scratch(width),
        compiler_params=params(),
        cost_estimate=pl.CostEstimate(flops=10**10, bytes_accessed=3 * 10**7, transcendentals=0),
        name="late",
    )(base, lists, counts, start, points, *arrived)


def shards(
    coords,
    vectors,
    basis,
    transfer,
    leaf_skeleton,
    device_skeleton,
    near_pairs,
    far_leaves,
    far_devices,
):
    col_count = lax.axis_size("col")
    row_here = lax.axis_index("row")
    col_here = lax.axis_index("col")
    rank_size = basis.shape[0]
    vec_count, points = vectors.shape
    leaves = transfer.shape[1] // rank_size
    leaf_width = points // leaves

    vec_left, vec_right = exchange(vectors, "col")
    vec_up, vec_down = exchange(vectors, "row")
    listed = near_pairs.shape[1]
    pairs_rows = jnp.pad(near_pairs.astype(F32), ((0, 1), (0, 0)))
    extra = jnp.concatenate([coords, leaf_skeleton, pairs_rows], axis=1)
    extra_left, extra_right = exchange(extra, "col")
    codes = [
        decode(part[:2, -listed:], side, row_here, col_here, col_count, leaves)
        for part, side in ((near_pairs, 0), (extra_left, -1), (extra_right, 1))
    ]
    lists, counts, relay = plan(*[jnp.concatenate(part) for part in zip(*codes)], leaves)
    extra = jnp.stack([extra_left, extra, extra_right])[..., :-listed]
    above, below = exchange(extra, "row")
    extra = jnp.stack([above, extra, below])

    coeff_own = jnp.einsum(
        "vil,ril->vir",
        vectors.reshape(vec_count, leaves, leaf_width),
        basis.reshape(rank_size, leaves, leaf_width),
        preferred_element_type=F32,
    ).astype(BF16)
    coeff = coeff_own.reshape(vec_count, leaves * rank_size)
    above, below = exchange(coeff, "col")
    coeff = jnp.stack([above, coeff, below])
    above, below = exchange(coeff, "row")
    coeff = jnp.stack([above, coeff, below])

    middle = [vec_up, vectors, vec_down]
    total = near(0, leaves, OWN_COL, lists, counts, None, extra, middle, 5 * 10**10)

    transfer_mats = transfer.reshape(rank_size, leaves, rank_size)
    device_coeff = jnp.einsum(
        "vir,ris->vs", coeff_own.astype(F32), transfer_mats, precision=HIGH
    )
    rounds_here = (jnp.maximum(counts[5], counts[6]) + CAP - 1) // CAP
    sheet = jnp.concatenate(
        [
            device_coeff,
            device_skeleton,
            jnp.full((1, rank_size), rounds_here, F32),
        ]
    )
    sheets = gather_all(sheet, ("row", "col"))
    devices = sheets.shape[0]
    rounds = jnp.max(sheets[:, vec_count + 3, 0]).astype(I32)
    me = row_here * col_count + col_here
    chosen = sheets[(far_devices[0] - me) % devices]
    coupling_top = kernel_block(chosen[:, vec_count : vec_count + 3], device_skeleton[None])
    device_far = jnp.einsum("fvs,fst->vt", chosen[:, :vec_count], coupling_top, precision=HIGH)

    coeff_pad = coeff.reshape(9, vec_count, leaves, rank_size)
    skeleton_pool = extra[..., points:].reshape(9, 3, leaves, rank_size)
    owner = far_leaves // leaves
    far_hood = (owner // col_count - row_here + 1) * 3 + owner % col_count - col_here + 1
    far_leaf = far_leaves % leaves
    picked_coeff = coeff_pad[far_hood, :, far_leaf, :].astype(F32)
    picked_skel = skeleton_pool[far_hood, :, far_leaf, :]
    own_skel = jnp.transpose(leaf_skeleton.reshape(3, leaves, rank_size), (1, 0, 2))
    coupling = kernel_block(picked_skel, own_skel[:, None])
    leaf_far = jnp.einsum("ifvs,ifst->ivt", picked_coeff, coupling, precision=HIGH)
    field = leaf_far + jnp.einsum("vs,ris->ivr", device_far, transfer_mats, precision=HIGH)
    far_part = jnp.einsum(
        "ivr,ril->vil",
        field.astype(BF16),
        basis.reshape(rank_size, leaves, leaf_width),
        preferred_element_type=F32,
    ).reshape(vec_count, points)

    total = near(
        1, leaves, ((1, 0), (1, 2)), lists, counts, total, extra, [vec_left, vec_right], 3 * 10**10
    )
    corners = [*exchange(vec_left, "row"), *exchange(vec_right, "row")]
    corner_spots = ((0, 0), (2, 0), (0, 2), (2, 2))
    total = near(2, leaves, corner_spots, lists, counts, total, extra, corners, 3 * 10**10)
    pools = [corners[0], vec_left, corners[1], corners[2], vec_right, corners[3]]

    def relay_round(index, total):
        base = (index * CAP).reshape(1)
        rows = relays(leaves, base, relay, extra, pools)
        arrived = [shift(rows[0], "col", 1), shift(rows[1], "col", -1)]
        return late(leaves, base, lists, counts, total, extra, arrived)

    total = relay_round(jnp.zeros((), I32), total)
    _, total = lax.while_loop(
        lambda state: state[0] < rounds,
        lambda state: (state[0] + 1, relay_round(*state)),
        (jnp.ones((), I32), total),
    )
    from_below = shift(total[0].astype(BF16), "row", -1)
    from_above = shift(total[2].astype(BF16), "row", 1)
    return total[1] + from_below.astype(F32) + from_above.astype(F32) + far_part


def solution(mesh):
    spread = P(None, ("row", "col"))
    lists = P(("row", "col"), None)
    in_specs = (spread,) * 7 + (lists,) * 2

    return jax.shard_map(shards, mesh=mesh, in_specs=in_specs, out_specs=spread, check_vma=False)
```

```python
import functools
import math

import jax
import jax.numpy as jnp
from jax import lax
from jax.experimental import pallas as pl
from jax.experimental.pallas import tpu as pltpu
from jax.sharding import PartitionSpec as P

HIGH = lax.Precision.HIGHEST
F32, BF16, I32 = jnp.float32, jnp.bfloat16, jnp.int32
CAP = 32
GROUP = 4
SHIFT = 4096
SMEM = pl.BlockSpec(memory_space=pltpu.SMEM)
VMEM = pl.BlockSpec(memory_space=pltpu.VMEM)
ANY = pl.BlockSpec(memory_space=pl.ANY)


def params(**more):
    return pltpu.CompilerParams(vmem_limit_bytes=58 * 1024 * 1024, **more)


def shift(block, axis, step):
    devices = range(lax.axis_size(axis))
    route = [(i, i + step) for i in devices if i + step in devices]
    return lax.ppermute(block, axis, route)


def exchange(block, axis):
    return shift(block, axis, 1), shift(block, axis, -1)


def gather_all(block, axes):
    count = lax.axis_size(axes)
    have, held = 1, block[None]
    while have < count:
        take = min(have, count - have)
        route = [(i, (i - have) % count) for i in range(count)]
        held = jnp.concatenate([held, lax.ppermute(held[:take], axes, route)])
        have += take
    return held


def kernel_block(left, right):
    total = None
    for dimension in range(3):
        gap = left[..., dimension, :, None] - right[..., dimension, None, :]
        total = gap * gap if total is None else total + gap * gap
    return jnp.exp(-0.5 * total)


def scaled(points):
    shifted = (points - 3.0) * math.sqrt(math.log2(math.e))
    return jnp.concatenate([shifted, jnp.zeros((8 - points.shape[0], points.shape[1]), F32)])


def split_rows(points, target):
    row = lax.broadcasted_iota(I32, points.shape, 0)
    half = -0.5 * jnp.sum(points * points, axis=0, keepdims=True)
    norm_row, one_row = (4, 3) if target else (3, 4)
    rest = jnp.where(row == norm_row, half, jnp.where(row == one_row, 1.0, points))
    parts = []
    for _ in range(3):
        part = rest.astype(BF16).astype(F32)
        rest = rest - part
        parts.append(part)
    high, middle, low = parts
    if target:
        order = (high, middle, low, high, middle, high)
    else:
        order = (high, high, high, middle, middle, low)
    return jnp.concatenate(order).astype(BF16)


def decode(pairs, side, row, col, cols, leaves):
    target, source = pairs[0].astype(I32), pairs[1].astype(I32)

    def split(leaf):
        owner = leaf // leaves
        return owner // cols - row, owner % cols - col, leaf % leaves

    t_row, t_col, t_leaf = split(target)
    s_row, s_col, s_leaf = split(source)
    into = (t_row + 1) * leaves + t_leaf
    out = (s_row + 1) * leaves + s_leaf
    exists = (col + side >= 0) & (col + side < cols)
    here = (t_col == 0) & exists
    beside = jnp.abs(s_col) == 1
    which = jnp.where(s_col == 0, 0, jnp.where(beside, jnp.where(s_row == 0, 1, 2), 4))
    if side == 0:
        which = jnp.where(here, which, 4)
        way = jnp.where((t_col == 1) & (s_col == -1), 0, -1)
        way = jnp.where((t_col == -1) & (s_col == 1), 1, way)
    else:
        far = here & (s_col == 2 * side)
        which = jnp.where(here, jnp.where(far, 4, which), 4)
        way = jnp.where(far, 2 if side == -1 else 3, -1)
    side_of = jnp.where(s_col == 1, 1, 0)
    part = jnp.where(which == 0, s_row + 1, side_of)
    part = jnp.where(which == 2, 2 * side_of + jnp.where(s_row == 1, 1, 0), part)
    entry = into * SHIFT + part * leaves + s_leaf
    key = jnp.where(way < 0, -1, way * 3 * leaves + out)
    return which, entry, key


def plan_kernel(leaves, which, entries, keys, lists, counts, relay, slots):
    pairs = entries.shape[0]
    reach = relay.shape[0] // 2

    def fill(ref, value):
        @pl.loop(0, ref.shape[0], unroll=8)
        def _(i):
            ref[i] = value

    fill(slots, -1)
    fill(relay, 0)

    def sort(p, found):
        group = which[p]
        at = jnp.where(group == 0, found[0], jnp.where(group == 1, found[1], found[2]))
        lists[group * pairs + at] = entries[p]
        return tuple(found[i] + jnp.where(group == i, 1, 0) for i in range(3))

    found = lax.fori_loop(0, pairs, sort, (0, 0, 0), unroll=8)
    for i in range(3):
        counts[i] = found[i]
    for i in range(3, counts.shape[0]):
        counts[i] = 0

    def note(p):
        key = keys[p]

        @pl.when(key >= 0)
        def _():
            way = lax.div(key, 3 * leaves)
            fresh = slots[key] < 0

            @pl.when(fresh)
            def _():
                slot = counts[5 + way]
                slots[key] = slot
                counts[5 + way] = slot + 1

                @pl.when(way < 2)
                def _():
                    relay[way * reach + slot] = lax.rem(key, 3 * leaves)

            @pl.when(way >= 2)
            def _():
                last = counts[3]
                target = lax.div(entries[p], SHIFT)
                lists[3 * pairs + last] = target * SHIFT + (way - 2) * 2048 + slots[key]
                counts[3] = last + 1

    @pl.loop(0, pairs, step=8)
    def _(p):
        top = keys[p]
        for i in range(1, 8):
            top = jnp.maximum(top, keys[p + i])

        @pl.when(top >= 0)
        def _():
            for i in range(8):
                note(p + i)


def plan(which, entries, keys, leaves):
    pairs = entries.shape[0]
    return pl.pallas_call(
        functools.partial(plan_kernel, leaves),
        out_shape=(
            jax.ShapeDtypeStruct((5 * pairs,), I32),
            jax.ShapeDtypeStruct((16,), I32),
            jax.ShapeDtypeStruct((2 * (pairs + CAP),), I32),
        ),
        in_specs=[SMEM] * 3,
        out_specs=(SMEM, SMEM, SMEM),
        scratch_shapes=[pltpu.SMEM((4 * 3 * leaves,), I32)],
        cost_estimate=pl.CostEstimate(flops=10**10, bytes_accessed=10**5, transcendentals=0),
        name="plan",
    )(which, entries, keys)


def pipeline(count, total, make, take, blocks):
    @pl.when(count > 0)
    def _():
        def fill(group, buffers):
            for i in range(GROUP):
                buffers[i] = make(jnp.minimum(group * GROUP + i, count - 1))

        def drain(group, buffers):
            values = []
            for i in range(GROUP):
                index = group * GROUP + i
                rows, spot, keep = take(jnp.minimum(index, count - 1))
                keep = jnp.where(index < count, keep, 0.0)
                value = jnp.dot(rows, buffers[i], preferred_element_type=F32)
                values.append((spot, value * keep))
            for (part, span), value in values:
                total[part, :, span] += value

        even, odd = blocks
        fill(0, even)

        @pl.loop(0, (count + 2 * GROUP - 1) // (2 * GROUP))
        def _(step):
            fill(2 * step + 1, odd)
            drain(2 * step, even)
            fill(2 * step + 2, even)
            drain(2 * step + 1, odd)


def spot_of(flat, leaves, width):
    return lax.div(flat, leaves), pl.ds(pl.multiple_of(lax.rem(flat, leaves) * width, width), width)


def matrix(source, target):
    exponent = lax.dot_general(
        source, target, (((0,), (0,)), ((), ())), preferred_element_type=F32
    )
    return jnp.exp2(exponent).astype(BF16)


def features(points, spots, out, target, leaves):
    width = out.shape[2] // leaves

    @pl.loop(0, leaves)
    def _(leaf):
        span = pl.ds(pl.multiple_of(leaf * width, width), width)
        for i, (row, col) in enumerate(spots):
            out[i, :, span] = split_rows(scaled(points[row, col, :, span]), target)


OWN_COL = ((0, 1), (1, 1), (2, 1))


def near_kernel(which, leaves, spots, fresh, *refs):
    lists, counts, *refs = refs
    if not fresh:
        start, *refs = refs
    points, *refs = refs
    pools = refs[:-7]
    out, pool, sources, targets, sems, *blocks = refs[-7:]
    length = pool.shape[2]
    width = length // leaves
    many = pool.shape[0]
    copies, place = [], 0
    for i, piece in enumerate(pools):
        span = pl.ds(place, piece.shape[1])
        copies.append(
            pltpu.make_async_copy(piece, pool.at[i * many // len(pools), :, span], sems.at[i])
        )
        place = (place + piece.shape[1]) % length
    if not fresh:
        copies.append(pltpu.make_async_copy(start, out, sems.at[len(pools)]))
    for copy in copies:
        copy.start()
    features(points, OWN_COL, targets, True, leaves)
    features(points, spots, sources, False, leaves)
    if fresh:

        @pl.loop(0, leaves)
        def _(leaf):
            span = pl.ds(pl.multiple_of(leaf * width, width), width)
            for i in range(3):
                out[i, :, span] = jnp.zeros((out.shape[1], width), F32)

    for copy in copies:
        copy.wait()
    begin = which * (lists.shape[0] // 5)

    def make(i):
        packed = lists[begin + i]
        t_part, t_span = spot_of(lax.div(packed, SHIFT), leaves, width)
        s_part, s_span = spot_of(lax.rem(packed, SHIFT), leaves, width)
        return matrix(sources[s_part, :, s_span], targets[t_part, :, t_span])

    def take(i):
        packed = lists[begin + i]
        s_part, s_span = spot_of(lax.rem(packed, SHIFT), leaves, width)
        return pool[s_part, :, s_span], spot_of(lax.div(packed, SHIFT), leaves, width), 1.0

    pipeline(counts[which], out, make, take, blocks)


def block_scratch(width):
    return [pltpu.VMEM((GROUP, width, width), BF16)] * 2


def near(which, leaves, spots, lists, counts, start, points, pools, cost):
    many = len(pools)
    pools = [piece for pool in pools for piece in pool]
    rows, length = pools[0].shape[0], sum(piece.shape[1] for piece in pools) // many
    first = [] if start is None else [start]
    return pl.pallas_call(
        functools.partial(near_kernel, which, leaves, spots, start is None),
        out_shape=jax.ShapeDtypeStruct((3, rows, length), F32),
        in_specs=[SMEM, SMEM] + [ANY] * len(first) + [VMEM] + [ANY] * len(pools),
        out_specs=VMEM,
        scratch_shapes=[
            pltpu.VMEM((many, rows, length), BF16),
            pltpu.VMEM((many, 48, length), BF16),
            pltpu.VMEM((3, 48, length), BF16),
            pltpu.SemaphoreType.DMA((len(pools) + 1,)),
        ]
        + block_scratch(length // leaves),
        compiler_params=params(),
        cost_estimate=pl.CostEstimate(flops=cost, bytes_accessed=3 * 10**7, transcendentals=0),
    )(lists, counts, *first, points, *pools)


def relay_kernel(leaves, base, relay, points, *refs):
    pools, (outs, sems) = refs[:-3], (refs[-3:-1], refs[-1])
    chunks = len(pools) // 6
    height, width = pools[0].shape[0], outs[0].shape[2]
    begin = base[0]
    reach = relay.shape[0] // 2

    for way in range(2):

        @pl.loop(0, CAP)
        def _(i):
            flat = relay[way * reach + begin + i]
            part, leaf = lax.div(flat, leaves), lax.rem(flat, leaves)
            for option in range(3):
                first = 0
                for chunk in range(chunks):
                    source = pools[(way * 3 + option) * chunks + chunk]
                    last = first + source.shape[1] // width

                    @pl.when((part == option) & (leaf >= first) & (leaf < last))
                    def _():
                        span = pl.ds(pl.multiple_of((leaf - first) * width, width), width)
                        pltpu.make_async_copy(
                            source.at[:, span], outs[way].at[i, :height], sems.at[way, i]
                        ).start()

                    first = last

            span = pl.ds(pl.multiple_of(leaf * width, width), width)
            rest = scaled(points[part, 2 * way, :, span])
            parts = []
            for _ in range(3):
                parts.append(rest.astype(BF16).astype(F32))
                rest = rest - parts[-1]
            high = parts[0] + pltpu.roll(parts[2], 5, 0)
            outs[way][i, height:] = jnp.concatenate([high, parts[1]]).astype(BF16)

    for way in range(2):

        @pl.loop(0, CAP)
        def _(i):
            pltpu.make_async_copy(
                pools[0].at[:, :width], outs[way].at[i, :height], sems.at[way, i]
            ).wait()


def relays(leaves, base, relay, points, pools):
    pools = [piece for pool in pools for piece in pool]
    height, length = pools[0].shape[0], sum(piece.shape[1] for piece in pools) // 6
    width = length // leaves
    out = jax.ShapeDtypeStruct((CAP, height + 16, width), BF16)
    return pl.pallas_call(
        functools.partial(relay_kernel, leaves),
        out_shape=(out, out),
        in_specs=[SMEM, SMEM, VMEM] + [ANY] * len(pools),
        out_specs=(VMEM, VMEM),
        scratch_shapes=[pltpu.SemaphoreType.DMA((2, CAP))],
        compiler_params=params(),
        name="relays",
    )(base, relay, points, *pools)


def late_kernel(leaves, final, base, lists, counts, start, points, *refs):
    arrived, refs = refs[:2], refs[2:]
    if final:
        own, above, below, *refs = refs
    out, sources, targets, sem, *blocks = refs
    height, length = out.shape[1:]
    width = length // leaves
    copy = pltpu.make_async_copy(start, out, sem)
    copy.start()
    features(points, OWN_COL, targets, True, leaves)
    for way in range(2):

        @pl.loop(0, CAP)
        def _(i):
            rows = arrived[way][i, height:].astype(F32)
            high, middle = rows[:8], rows[8:]
            row = lax.broadcasted_iota(I32, high.shape, 0)
            low = pltpu.roll(high, 3, 0)
            exact = jnp.where(row < 3, high + middle + low, 0.0)
            sources[way, i] = split_rows(exact, False)

    copy.wait()
    begin = base[0]
    skip = 3 * (lists.shape[0] // 5)

    def slot_of(packed):
        slot = lax.rem(packed, 2048) - begin
        inside = jnp.clip(slot, 0, CAP - 1)
        return lax.div(lax.rem(packed, SHIFT), 2048), inside, jnp.where(slot == inside, 1.0, 0.0)

    def make(i):
        packed = lists[skip + i]
        way, slot, _ = slot_of(packed)
        t_part, t_span = spot_of(lax.div(packed, SHIFT), leaves, width)
        return matrix(sources[way, slot], targets[t_part, :, t_span])

    def take(i):
        packed = lists[skip + i]
        way, slot, keep = slot_of(packed)
        rows = jnp.where(way == 0, arrived[0][slot, :height], arrived[1][slot, :height])
        return rows, spot_of(lax.div(packed, SHIFT), leaves, width), keep

    pipeline(counts[3], out, make, take, blocks)
    if final:

        @pl.loop(0, leaves)
        def _(leaf):
            span = pl.ds(pl.multiple_of(leaf * width, width), width)
            above[:, span] = out[0, :, span].astype(BF16)
            own[:, span] = out[1, :, span]
            below[:, span] = out[2, :, span].astype(BF16)


def late(leaves, final, base, lists, counts, start, points, arrived):
    _, rows, length = start.shape
    width = length // leaves
    shape = jax.ShapeDtypeStruct(start.shape, F32)
    scratch = []
    if final:
        scratch = [pltpu.VMEM(start.shape, F32)]
        shape = tuple(jax.ShapeDtypeStruct((rows, length), kind) for kind in (F32, BF16, BF16))
    return pl.pallas_call(
        functools.partial(late_kernel, leaves, final),
        out_shape=shape,
        in_specs=[SMEM] * 3 + [ANY] + [VMEM] * 3,
        out_specs=(VMEM,) * 3 if final else VMEM,
        scratch_shapes=scratch
        + [
            pltpu.VMEM((2, CAP, 48, width), BF16),
            pltpu.VMEM((3, 48, start.shape[2]), BF16),
            pltpu.SemaphoreType.DMA,
        ]
        + block_scratch(width),
        compiler_params=params(),
        cost_estimate=pl.CostEstimate(flops=10**10, bytes_accessed=3 * 10**7, transcendentals=0),
        name="late" if final else "later",
    )(base, lists, counts, start, points, *arrived)


def shards(
    coords,
    vectors,
    basis,
    transfer,
    leaf_skeleton,
    device_skeleton,
    near_pairs,
    far_leaves,
    far_devices,
):
    col_count = lax.axis_size("col")
    row_here = lax.axis_index("row")
    col_here = lax.axis_index("col")
    rank_size = basis.shape[0]
    vec_count, points = vectors.shape
    leaves = transfer.shape[1] // rank_size
    leaf_width = points // leaves

    cut = leaves * 3 // 4 * leaf_width
    pieces = [vectors[:, :cut], vectors[:, cut:]]
    vec_left, vec_right = zip(*[exchange(piece, "col") for piece in pieces])
    vec_up, vec_down = exchange(vectors, "row")
    listed = near_pairs.shape[1]
    pairs_rows = jnp.pad(near_pairs.astype(F32), ((0, 1), (0, 0)))
    extra = jnp.concatenate([coords, leaf_skeleton, pairs_rows], axis=1)
    extra_left, extra_right = exchange(extra, "col")
    codes = [
        decode(part[:2, -listed:], side, row_here, col_here, col_count, leaves)
        for part, side in ((near_pairs, 0), (extra_left, -1), (extra_right, 1))
    ]
    lists, counts, relay = plan(*[jnp.concatenate(part) for part in zip(*codes)], leaves)
    extra = jnp.stack([extra_left, extra, extra_right])[..., :-listed]
    above, below = exchange(extra, "row")
    extra = jnp.stack([above, extra, below])

    coeff_own = jnp.einsum(
        "vil,ril->vir",
        vectors.reshape(vec_count, leaves, leaf_width),
        basis.reshape(rank_size, leaves, leaf_width),
        preferred_element_type=F32,
    ).astype(BF16)
    coeff = coeff_own.reshape(vec_count, leaves * rank_size)
    above, below = exchange(coeff, "col")
    coeff = jnp.stack([above, coeff, below])
    above, below = exchange(coeff, "row")
    coeff = jnp.stack([above, coeff, below])

    middle = [[vec_up], [vectors], [vec_down]]
    total = near(0, leaves, OWN_COL, lists, counts, None, extra, middle, 5 * 10**10)

    transfer_mats = transfer.reshape(rank_size, leaves, rank_size)
    device_coeff = jnp.einsum(
        "vir,ris->vs", coeff_own.astype(F32), transfer_mats, precision=HIGH
    )
    rounds_here = (jnp.maximum(counts[5], counts[6]) + CAP - 1) // CAP
    sheet = jnp.concatenate(
        [
            device_coeff,
            device_skeleton,
            jnp.full((1, rank_size), rounds_here, F32),
        ]
    )
    sheets = gather_all(sheet, ("row", "col"))
    devices = sheets.shape[0]
    rounds = jnp.max(sheets[:, vec_count + 3, 0]).astype(I32)
    me = row_here * col_count + col_here
    chosen = sheets[(far_devices[0] - me) % devices]
    coupling_top = kernel_block(chosen[:, vec_count : vec_count + 3], device_skeleton[None])
    device_far = jnp.einsum("fvs,fst->vt", chosen[:, :vec_count], coupling_top, precision=HIGH)

    coeff_pad = coeff.reshape(9, vec_count, leaves, rank_size)
    skeleton_pool = extra[..., points:].reshape(9, 3, leaves, rank_size)
    owner = far_leaves // leaves
    far_hood = (owner // col_count - row_here + 1) * 3 + owner % col_count - col_here + 1
    far_leaf = far_leaves % leaves
    picked_coeff = coeff_pad[far_hood, :, far_leaf, :].astype(F32)
    picked_skel = skeleton_pool[far_hood, :, far_leaf, :]
    own_skel = jnp.transpose(leaf_skeleton.reshape(3, leaves, rank_size), (1, 0, 2))
    coupling = kernel_block(picked_skel, own_skel[:, None])
    leaf_far = jnp.einsum("ifvs,ifst->ivt", picked_coeff, coupling, precision=HIGH)
    field = leaf_far + jnp.einsum("vs,ris->ivr", device_far, transfer_mats, precision=HIGH)
    far_part = jnp.einsum(
        "ivr,ril->vil",
        field.astype(BF16),
        basis.reshape(rank_size, leaves, leaf_width),
        preferred_element_type=F32,
    ).reshape(vec_count, points)

    total = near(
        1, leaves, ((1, 0), (1, 2)), lists, counts, total, extra, [vec_left, vec_right], 3 * 10**10
    )
    corners = []
    for side in (vec_left, vec_right):
        corners += zip(*[exchange(piece, "row") for piece in side])
    corner_spots = ((0, 0), (2, 0), (0, 2), (2, 2))
    total = near(2, leaves, corner_spots, lists, counts, total, extra, corners, 3 * 10**10)
    pools = [corners[0], vec_left, corners[1], corners[2], vec_right, corners[3]]

    def relay_round(index, total, final):
        base = (index * CAP).reshape(1)
        up, down = relays(leaves, base, relay, extra, pools)
        arrived = [shift(up, "col", 1), shift(down, "col", -1)]
        return late(leaves, final, base, lists, counts, total, extra, arrived)

    _, total = lax.while_loop(
        lambda state: state[0] < rounds,
        lambda state: (state[0] + 1, relay_round(*state, False)),
        (jnp.ones((), I32), total),
    )
    own, above, below = relay_round(jnp.zeros((), I32), total, True)
    from_below = shift(above, "row", -1)
    from_above = shift(below, "row", 1)
    return own + from_below.astype(F32) + from_above.astype(F32) + far_part


def solution(mesh):
    spread = P(None, ("row", "col"))
    lists = P(("row", "col"), None)
    in_specs = (spread,) * 7 + (lists,) * 2

    return jax.shard_map(shards, mesh=mesh, in_specs=in_specs, out_specs=spread, check_vma=False)
```
